32 devices in a mesh: section: 2 (over x), dp: 4 (over y, core), tensor: 4 (over z).
Axes of the slice: x: 2, y: 2, z: 4, core: 2. Of those that a mesh axis runs over, the one named last changes fastest.
Arguments:
- block_input: bfloat16 [2, 4, 256, 1024], P(None, 'dp', 'tensor'), may hold values from -6 to 6
- seq_ids: int32 [2, 4, 256], P(None, 'dp'), may hold values from 0 to 7, never falling along the last dimension, each value on 1 to 192 neighbouring positions
- out_cotangent: bfloat16 [2, 4, 256, 1024], P(None, 'dp', 'tensor'), may hold values from -6 to 6
- qkv_weight: bfloat16 [2, 1024, 3, 1024], P('section', 'dp', None, 'tensor'), may hold values from -0.1875 to 0.1875
- qv_bias: bfloat16 [2, 2, 16, 64], P('section', None, 'tensor', 'dp'), may hold values from -3 to 3
- out_weight: bfloat16 [2, 1024, 1024], P('section', 'tensor', 'dp'), may hold values from -0.5 to 0.5
- out_bias: bfloat16 [2, 1024], P('section', 'dp'), may hold values from -3 to 3
- norm1_gain: bfloat16 [2, 1024], P('section', 'dp'), may hold values from 0.25 to 1.75
- norm1_bias: bfloat16 [2, 1024], P('section', 'dp'), may hold values from -3 to 3
- up_weight: bfloat16 [2, 1024, 4096], P('section', 'dp', 'tensor'), may hold values from -0.1875 to 0.1875
- up_bias: bfloat16 [2, 16, 256], P('section', 'tensor', 'dp'), may hold values from -3 to 3
- down_weight: bfloat16 [2, 4096, 1024], P('section', 'tensor', 'dp'), may hold values from -0.09375 to 0.09375
- down_bias: bfloat16 [2, 1024], P('section', 'dp'), may hold values from -3 to 3
- norm2_gain: bfloat16 [2, 1024], P('section', 'dp'), may hold values from 0.25 to 1.75
- norm2_bias: bfloat16 [2, 1024], P('section', 'dp'), may hold values from -3 to 3
Outputs:
- section_outputs: bfloat16 [2, 2, 4, 256, 1024], P('section', None, 'dp', 'tensor')
- input_grads: float32 [2, 2, 4, 256, 1024], P('section', None, 'dp', 'tensor')
- qkv_weight_grad: float32 [2, 1024, 3, 1024], P('section', 'dp', None, 'tensor')
- qv_bias_grad: float32 [2, 2, 16, 64], P('section', None, 'tensor', 'dp')
- out_weight_grad: float32 [2, 1024, 1024], P('section', 'tensor', 'dp')
- out_bias_grad: float32 [2, 1024], P('section', ('dp', 'tensor'))
- norm1_gain_grad: float32 [2, 1024], P('section', ('dp', 'tensor'))
- norm1_bias_grad: float32 [2, 1024], P('section', ('dp', 'tensor'))
- up_weight_grad: float32 [2, 1024, 4096], P('section', 'dp', 'tensor')
- up_bias_grad: float32 [2, 16, 256], P('section', 'tensor', 'dp')
- down_weight_grad: float32 [2, 4096, 1024], P('section', 'tensor', 'dp')
- down_bias_grad: float32 [2, 1024], P('section', ('dp', 'tensor'))
- norm2_gain_grad: float32 [2, 1024], P('section', ('dp', 'tensor'))
- norm2_bias_grad: float32 [2, 1024], P('section', ('dp', 'tensor'))
The draws below stay inside these ranges and needn't reach their ends.
Inputs may be any that keep to these rules, and one draw needn't show every extreme that they name: `seq_ids`: along each pack of 256 tokens the ids never fall; every sequence has 1 to 192 tokens and one of each pack has exactly 192.
All inputs are finite; a program needn't handle non-finite values.
Results may differ from the reference program's by a relative error of at most 0.029.
Values may be sent and summed in bfloat16 or wider, within the bound.
A program may use at most 128 MiB of HBM per device.

```python
import math
import jax
import jax.numpy as jnp
import numpy as np
from jax import lax

D = 1024
FF = 4096
H = 16
HD = 64
MB = 2
TOK_MB = 256
PACKS = 4
SEQ_MAX = 192
SEQS = 8


def level_of(key, shape, shards, smallest, high):
    factor_of = 1.0
    for axis_at, parts in shards:
        steps = jax.random.uniform(jax.random.fold_in(jax.random.fold_in(key, 6), axis_at), (parts,), jnp.float32, smallest / len(shards), high / len(shards))
        factor_of = factor_of * jnp.repeat(jnp.exp(steps), shape[axis_at] // parts).reshape((-1,) + (1,) * (len(shape) - 1 - axis_at))
    return factor_of


def length_profile(amount, total, limit, lean):
    weights = [(1 << 20) // math.isqrt(grade ** lean) + 1 for grade in range(2, amount + 1)]
    spare, given = total - limit - (amount - 1), [1] * (amount - 1)
    while spare > 0:
        movable = [i for i in range(amount - 1) if given[i] < limit]
        pool, budget = sum([weights[i] for i in movable]), spare
        for i in movable:
            more = min(limit - given[i], max(1, budget * weights[i] // pool), spare)
            given[i] = given[i] + more
            spare = spare - more
    return np.array([limit] + given)


def ragged(own_key, amount, total, bound, skew):
    if amount == 2:
        one = jax.random.randint(own_key, (), max(1, total - bound), min(bound, total - 1) + 1)
        return jnp.stack([one, total - one])
    sizes = jnp.asarray(length_profile(amount, total, bound, skew), jnp.int32)
    twos = (amount - 1) // 2
    giver, sink = sizes[1:1 + 2 * twos:2], sizes[2:2 + 2 * twos:2]
    room = jnp.minimum(giver - 1, bound - sink)
    moved = jax.random.randint(jax.random.fold_in(own_key, 1), (twos,), 0, 1 << 20) % (room + 1)
    sizes = sizes.at[1:1 + 2 * twos:2].set(giver - moved).at[2:2 + 2 * twos:2].set(sink + moved)
    return sizes[jax.random.permutation(jax.random.fold_in(own_key, 2), amount)]


def noise(own_key, dims, scale, limit, split=(), kind=jnp.bfloat16):
    entries = scale * jax.random.normal(own_key, dims, jnp.float32)
    if split:
        entries = entries * level_of(own_key, dims, split, -0.22, 0.18)
    return jnp.clip(entries, -limit, limit).astype(kind)


def setup_inputs(seed: int = 0) -> dict:
    key_of = jax.random.split(jax.random.key(seed), 16)
    block_input = noise(key_of[0], (MB, PACKS, TOK_MB, D), 1.0, 6.0, ((1, 4), (2, 4)))
    seq_ids = jax.vmap(lambda own: jnp.searchsorted(jnp.cumsum(ragged(own, SEQS, TOK_MB, SEQ_MAX, 2)), jnp.arange(TOK_MB), side="right"))(jax.random.split(key_of[1], MB * PACKS)).reshape((MB, PACKS, TOK_MB)).astype(jnp.int32)
    out_cotangent = noise(key_of[2], (MB, PACKS, TOK_MB, D), 1.0, 6.0, ((1, 4), (2, 4)))
    qkv_weight = noise(key_of[3], (2, D, 3, D), D ** -0.5, 0.1875, ((0, 2), (1, 4), (3, 4)))
    qv_bias = noise(key_of[4], (2, 2, H, HD), 0.5, 3.0, ((0, 2), (2, 4), (3, 4)))
    out_weight = noise(key_of[5], (2, D, D), (D // 8) ** -0.5, 0.5, ((0, 2), (1, 4), (2, 4)))
    out_bias = noise(key_of[6], (2, D), 0.5, 3.0, ((0, 2), (1, 4)))
    norm1_gain = jnp.clip(1.0 + 0.15 * jax.random.normal(key_of[7], (2, D), jnp.float32), 0.25, 1.75).astype(jnp.bfloat16)
    norm1_bias = noise(key_of[8], (2, D), 0.5, 3.0, ((0, 2), (1, 4)))
    up_weight = noise(key_of[9], (2, D, FF), D ** -0.5, 0.1875, ((0, 2), (1, 4), (2, 4)))
    up_bias = noise(key_of[10], (2, 16, FF // 16), 0.5, 3.0, ((0, 2), (1, 4), (2, 4)))
    down_weight = noise(key_of[11], (2, FF, D), FF ** -0.5, 0.09375, ((0, 2), (1, 4), (2, 4)))
    down_bias = noise(key_of[12], (2, D), 0.5, 3.0, ((0, 2), (1, 4)))
    norm2_gain = jnp.clip(1.0 + 0.15 * jax.random.normal(key_of[13], (2, D), jnp.float32), 0.25, 1.75).astype(jnp.bfloat16)
    norm2_bias = noise(key_of[14], (2, D), 0.5, 3.0, ((0, 2), (1, 4)))
    return dict(block_input=block_input, seq_ids=seq_ids, out_cotangent=out_cotangent, qkv_weight=qkv_weight, qv_bias=qv_bias, out_weight=out_weight, out_bias=out_bias, norm1_gain=norm1_gain, norm1_bias=norm1_bias, up_weight=up_weight, up_bias=up_bias, down_weight=down_weight, down_bias=down_bias, norm2_gain=norm2_gain, norm2_bias=norm2_bias)


def gelu_exact(values):
    return 0.5 * values * (1.0 + jax.scipy.special.erf(values * 0.7071067811865476))

def gelu_slope(values):
    return 0.5 * (1.0 + jax.scipy.special.erf(values * 0.7071067811865476)) + values * jnp.exp(-0.5 * values * values) * 0.3989422804014327

def to_wide(values):
    return lax.optimization_barrier(values.astype(jnp.bfloat16)).astype(jnp.float32)

def normalize(summed):
    center = summed - lax.optimization_barrier(jnp.mean(summed, axis=-1, keepdims=True))
    scaled = lax.rsqrt(lax.optimization_barrier(jnp.mean(center * center, axis=-1, keepdims=True)) + 1e-12)
    return (center * scaled, scaled)

def norm_back(upstream, normed, scaled):
    return scaled * (upstream - lax.optimization_barrier(jnp.mean(upstream, axis=-1, keepdims=True)) - normed * lax.optimization_barrier(jnp.mean(upstream * normed, axis=-1, keepdims=True)))

def masked_probs(queries, keys, same_seq):
    scores = jnp.einsum('qhd,khd->hqk', queries, keys) * HD ** (-0.5)
    scores = jnp.where(same_seq[None], scores, -jnp.inf)
    largest = lax.optimization_barrier(jnp.max(scores, axis=-1, keepdims=True))
    shifted = jnp.exp(scores - largest)
    return shifted / lax.optimization_barrier(jnp.sum(shifted, axis=-1, keepdims=True))

def layer_forward(inputs, same_seq, params):
    qkv_mat, qv_shift, out_mat, out_shift, gain_one, shift_one, up_mat, up_shift, down_mat, down_shift, gain_two, shift_two = params
    tokens = inputs.shape[0]
    inputs_wide = inputs.astype(jnp.float32)
    projected = jnp.einsum('tc,cjn->tjn', inputs_wide, qkv_mat.astype(jnp.float32))
    qv_wide = qv_shift.astype(jnp.float32).reshape(2, D)
    bias_rows = jnp.concatenate([qv_wide[0:1], jnp.zeros((1, D), jnp.float32), qv_wide[1:2]], axis=0)
    qkv_held = (projected + bias_rows[None]).astype(jnp.bfloat16)
    queries = qkv_held[:, 0].reshape(tokens, H, HD).astype(jnp.float32)
    keys = qkv_held[:, 1].reshape(tokens, H, HD).astype(jnp.float32)
    values = qkv_held[:, 2].reshape(tokens, H, HD).astype(jnp.float32)
    attn_prob = masked_probs(queries, keys, same_seq)
    context = jnp.einsum('hqk,khd->qhd', to_wide(attn_prob), values).reshape(tokens, D).astype(jnp.bfloat16)
    resid_one = inputs_wide + jnp.dot(context, out_mat, preferred_element_type=jnp.float32) + out_shift.astype(jnp.float32)
    normed_one, scaled_one = normalize(resid_one)
    hidden_one = normed_one * gain_one.astype(jnp.float32) + shift_one.astype(jnp.float32)
    hidden_held = hidden_one.astype(jnp.bfloat16)
    pre_act = jnp.dot(hidden_held, up_mat, preferred_element_type=jnp.float32) + up_shift.astype(jnp.float32).reshape(FF)
    activated = gelu_exact(pre_act).astype(jnp.bfloat16)
    resid_two = hidden_one + jnp.dot(activated, down_mat, preferred_element_type=jnp.float32) + down_shift.astype(jnp.float32)
    normed_two, scaled_two = normalize(resid_two)
    layer_out = (normed_two * gain_two.astype(jnp.float32) + shift_two.astype(jnp.float32)).astype(jnp.bfloat16)
    return (layer_out, (qkv_held, context, normed_one, scaled_one, hidden_held, pre_act, activated, normed_two, scaled_two))

def layer_backward(inputs, same_seq, params, saved, upstream):
    qkv_mat, qv_shift, out_mat, out_shift, gain_one, shift_one, up_mat, up_shift, down_mat, down_shift, gain_two, shift_two = params
    qkv_held, context, normed_one, scaled_one, hidden_held, pre_act, activated, normed_two, scaled_two = saved
    tokens = inputs.shape[0]
    queries = qkv_held[:, 0].reshape(tokens, H, HD).astype(jnp.float32)
    keys = qkv_held[:, 1].reshape(tokens, H, HD).astype(jnp.float32)
    values = qkv_held[:, 2].reshape(tokens, H, HD).astype(jnp.float32)
    grad_two = norm_back(upstream * gain_two.astype(jnp.float32), normed_two, scaled_two)
    grad_two_held = grad_two.astype(jnp.bfloat16)
    down_grad = jnp.dot(activated.T, grad_two_held, preferred_element_type=jnp.float32)
    grad_pre = jnp.dot(grad_two_held, down_mat.T, preferred_element_type=jnp.float32) * gelu_slope(pre_act)
    grad_pre_held = grad_pre.astype(jnp.bfloat16)
    up_grad = jnp.dot(hidden_held.T, grad_pre_held, preferred_element_type=jnp.float32)
    grad_hidden = grad_two + jnp.dot(grad_pre_held, up_mat.T, preferred_element_type=jnp.float32)
    grad_one = norm_back(grad_hidden * gain_one.astype(jnp.float32), normed_one, scaled_one)
    grad_one_held = grad_one.astype(jnp.bfloat16)
    out_grad = jnp.dot(context.T, grad_one_held, preferred_element_type=jnp.float32)
    grad_context = jnp.dot(grad_one_held, out_mat.T, preferred_element_type=jnp.float32).astype(jnp.bfloat16).reshape(tokens, H, HD).astype(jnp.float32)
    attn_prob = masked_probs(queries, keys, same_seq)
    grad_prob = jnp.einsum('qhd,khd->hqk', grad_context, values)
    row_dots = lax.optimization_barrier(jnp.sum(attn_prob * grad_prob, axis=-1, keepdims=True))
    grad_scores = to_wide(attn_prob * (grad_prob - row_dots) * HD ** (-0.5))
    grad_queries = jnp.einsum('hqk,khd->qhd', grad_scores, keys)
    grad_keys = jnp.einsum('hqk,qhd->khd', grad_scores, queries)
    grad_values = jnp.einsum('hqk,qhd->khd', to_wide(attn_prob), grad_context)
    qv_grad = jnp.stack([lax.optimization_barrier(jnp.sum(grad_queries, axis=0)), lax.optimization_barrier(jnp.sum(grad_values, axis=0))])
    grad_qkv = jnp.stack([grad_queries, grad_keys, grad_values], axis=1).reshape(tokens, 3, D).astype(jnp.bfloat16)
    qkv_grad = jnp.einsum('tc,tjn->cjn', inputs.astype(jnp.float32), grad_qkv.astype(jnp.float32))
    grad_inputs = grad_one + jnp.einsum('tjn,cjn->tc', grad_qkv.astype(jnp.float32), qkv_mat.astype(jnp.float32))
    row_grads = jnp.stack([lax.optimization_barrier(jnp.sum(grad_one, axis=0)), lax.optimization_barrier(jnp.sum(grad_hidden * normed_one, axis=0)), lax.optimization_barrier(jnp.sum(grad_hidden, axis=0)), lax.optimization_barrier(jnp.sum(grad_two, axis=0)), lax.optimization_barrier(jnp.sum(upstream * normed_two, axis=0)), lax.optimization_barrier(jnp.sum(upstream, axis=0))])
    up_shift_grad = lax.optimization_barrier(jnp.sum(grad_pre, axis=0)).reshape(16, FF // 16)
    return (grad_inputs, (qkv_grad, qv_grad, out_grad, up_grad, up_shift_grad, down_grad, row_grads))

def reference(block_input, seq_ids, out_cotangent, qkv_weight, qv_bias, out_weight, out_bias, norm1_gain, norm1_bias, up_weight, up_bias, down_weight, down_bias, norm2_gain, norm2_bias):

    def section_params(which):
        return (qkv_weight[which], qv_bias[which], out_weight[which], out_bias[which], norm1_gain[which], norm1_bias[which], up_weight[which], up_bias[which], down_weight[which], down_bias[which], norm2_gain[which], norm2_bias[which])
    first_params = section_params(0)
    second_params = section_params(1)
    pack_count = MB * PACKS
    inputs_all = block_input.reshape(pack_count, TOK_MB, D)
    ids_all = seq_ids.reshape(pack_count, TOK_MB)
    upstream_all = out_cotangent.reshape(pack_count, TOK_MB, D)
    grad_shapes = [(D, 3, D), (2, H, HD), (D, D), (D, FF), (16, FF // 16), (FF, D), (6, D)]
    initial = tuple((jnp.zeros((2,) + grad_shape, jnp.float32) for grad_shape in grad_shapes))

    def advance(totals, pack_item):
        inputs, pack_ids, upstream = pack_item
        same_seq = pack_ids[:, None] == pack_ids[None, :]
        middle, saved_first = layer_forward(inputs, same_seq, first_params)
        final_out, saved_second = layer_forward(middle, same_seq, second_params)
        grad_middle, from_second = layer_backward(middle, same_seq, second_params, saved_second, upstream.astype(jnp.float32))
        grad_inputs, from_first = layer_backward(inputs, same_seq, first_params, saved_first, grad_middle)
        totals = tuple((running + jnp.stack([early, later]) for running, early, later in zip(totals, from_first, from_second)))
        return (totals, (middle, final_out, grad_inputs, grad_middle))
    totals, (middles, finals, grad_firsts, grad_seconds) = lax.scan(advance, initial, (inputs_all, ids_all, upstream_all))
    section_outputs = jnp.stack([middles, finals]).reshape(2, MB, PACKS, TOK_MB, D)
    input_grads = jnp.stack([grad_firsts, grad_seconds]).reshape(2, MB, PACKS, TOK_MB, D)
    row_grads = totals[6]
    return (section_outputs, input_grads, totals[0], totals[1], totals[2], row_grads[:, 0], row_grads[:, 1], row_grads[:, 2], totals[3], totals[4], totals[5], row_grads[:, 3], row_grads[:, 4], row_grads[:, 5])
```

```python
import functools

import jax
import jax.numpy as jnp
from jax import lax
from jax.experimental import pallas as pl
from jax.experimental.pallas import tpu as pltpu
from jax.sharding import PartitionSpec as P

MESH = pl.DeviceIdType.MESH
F32 = jnp.float32
BF16 = jnp.bfloat16
VMEM_SPEC = pl.BlockSpec(memory_space=pltpu.VMEM)
VMEM_LIMIT = 60 * 1024 * 1024


def line_barrier(me, count):
    barrier = pltpu.get_barrier_semaphore()

    @pl.when(me > 0)
    def _():
        pl.semaphore_signal(barrier, inc=1, device_id={"tensor": me - 1}, device_id_type=MESH)

    @pl.when(me < count - 1)
    def _():
        pl.semaphore_signal(barrier, inc=1, device_id={"tensor": me + 1}, device_id_type=MESH)

    inner = jnp.logical_and(me > 0, me < count - 1)

    @pl.when(inner)
    def _():
        pl.semaphore_wait(barrier, 2)

    @pl.when(jnp.logical_not(inner))
    def _():
        pl.semaphore_wait(barrier, 1)


def gather_kernel(count, own_ref, all_ref, send_sem, recv_sem):
    me = lax.axis_index("tensor")
    line_barrier(me, count)

    def copy_of(side, step):
        shard = me - step if side == 0 else me + step
        target = me + 1 if side == 0 else me - 1
        return pltpu.make_async_remote_copy(
            src_ref=own_ref if step == 0 else all_ref.at[shard],
            dst_ref=all_ref.at[shard],
            send_sem=send_sem.at[side, step],
            recv_sem=recv_sem.at[side, step],
            device_id={"tensor": target},
            device_id_type=MESH,
        )

    def arrival(side, step):
        shard = me - step if side == 0 else me + step
        return pltpu.make_async_remote_copy(
            src_ref=all_ref.at[shard],
            dst_ref=all_ref.at[shard],
            send_sem=send_sem.at[side, step - 1],
            recv_sem=recv_sem.at[side, step - 1],
            device_id={"tensor": me - 1 if side == 0 else me + 1},
            device_id_type=MESH,
        )

    def holds(side, step):
        return me >= step if side == 0 else me + step <= count - 1

    def sends(side):
        return me < count - 1 if side == 0 else me > 0

    for step in range(count):
        for side in range(2):

            @pl.when(holds(side, step))
            def _():
                if step > 0:
                    arrival(side, step).wait_recv()
                if step < count - 1:

                    @pl.when(sends(side))
                    def _():
                        copy_of(side, step).start()

        if step == 0:
            all_ref[me] = own_ref[...]
    for step in range(count - 1):
        for side in range(2):

            @pl.when(holds(side, step))
            def _():
                @pl.when(sends(side))
                def _():
                    copy_of(side, step).wait_send()


def tensor_gather(rows):
    count = lax.axis_size("tensor")
    gathered = pl.pallas_call(
        functools.partial(gather_kernel, count),
        out_shape=jax.ShapeDtypeStruct((count,) + rows.shape, rows.dtype),
        in_specs=[VMEM_SPEC],
        out_specs=VMEM_SPEC,
        scratch_shapes=[
            pltpu.SemaphoreType.DMA((2, count - 1)),
            pltpu.SemaphoreType.DMA((2, count - 1)),
        ],
        compiler_params=pltpu.CompilerParams(collective_id=1, has_side_effects=True),
        name="tensor_gather",
    )(rows)
    return gathered.reshape(count * rows.shape[0], rows.shape[1])


def scatter_kernel(count, part_ref, sum_ref, landed, staged, send_sem, recv_sem):
    me = lax.axis_index("tensor")
    line_barrier(me, count)

    def copy_of(side, slot, first, dest):
        return pltpu.make_async_remote_copy(
            src_ref=part_ref.at[dest] if first else staged.at[side, slot],
            dst_ref=landed.at[side, slot],
            send_sem=send_sem.at[side, slot],
            recv_sem=recv_sem.at[side, slot],
            device_id={"tensor": me + 1 if side == 0 else me - 1},
            device_id_type=MESH,
        )

    def roles(side, slot):
        dest = count - 1 - slot if side == 0 else slot
        passes = me < dest if side == 0 else me > dest
        first = me == 0 if side == 0 else me == count - 1
        return dest, passes, first

    for slot in range(count - 1):
        for side in range(2):
            dest, passes, first = roles(side, slot)

            @pl.when(first)
            def _():
                copy_of(side, slot, True, dest).start()

    for slot in range(count - 1):
        for side in range(2):
            dest, passes, first = roles(side, slot)

            @pl.when(jnp.logical_and(passes, jnp.logical_not(first)))
            def _():
                copy_of(side, slot, False, dest).wait_recv()
                staged[side, slot] = (
                    part_ref[dest].astype(F32) + landed[side, slot].astype(F32)
                ).astype(BF16)
                copy_of(side, slot, False, dest).start()

    for place in range(count):

        @pl.when(me == place)
        def _():
            total = part_ref[place].astype(F32)
            if place > 0:
                copy_of(0, count - 1 - place, False, place).wait_recv()
                total = total + landed[0, count - 1 - place].astype(F32)
            if place < count - 1:
                copy_of(1, place, False, place).wait_recv()
                total = total + landed[1, place].astype(F32)
            sum_ref[...] = total

    for slot in range(count - 1):
        for side in range(2):
            dest, passes, first = roles(side, slot)

            @pl.when(passes)
            def _():
                copy_of(side, slot, False, dest).wait_send()


def tensor_scatter(parts):
    count = lax.axis_size("tensor")
    rows = parts.shape[0] // count
    width = parts.shape[1]
    return pl.pallas_call(
        functools.partial(scatter_kernel, count),
        out_shape=jax.ShapeDtypeStruct((rows, width), F32),
        in_specs=[VMEM_SPEC],
        out_specs=VMEM_SPEC,
        scratch_shapes=[
            pltpu.VMEM((2, count - 1, rows, width), BF16),
            pltpu.VMEM((2, count - 1, rows, width), BF16),
            pltpu.SemaphoreType.DMA((2, count - 1)),
            pltpu.SemaphoreType.DMA((2, count - 1)),
        ],
        compiler_params=pltpu.CompilerParams(collective_id=2, has_side_effects=True),
        name="tensor_scatter",
    )(parts.reshape(count, rows, width))


class Cube:
    def __init__(self, dp_count):
        self.dp_count = dp_count
        self.dp_bits = dp_count.bit_length() - 1
        self.bits = self.dp_bits + 1
        self.size = 2 * dp_count
        self.section = lax.axis_index("section")
        self.dp = lax.axis_index("dp")

    def place(self, mask):
        section = 1 - self.section if mask & self.dp_count else self.section
        dp = self.dp
        for bit in range(self.dp_bits):
            if mask & (1 << bit):
                dp = dp + (1 << bit) * (1 - 2 * ((self.dp // (1 << bit)) % 2))
        return section, dp

    def device(self, mask):
        section, dp = self.place(mask)
        return {"section": section, "dp": dp}

    def order(self, kind):
        bits = list(range(self.bits - 1, -1, -1))
        if kind:
            bits[0], bits[1] = bits[1], bits[0]
        return bits

    def greet(self, others=()):
        barrier = pltpu.get_barrier_semaphore()
        targets = [self.device(1 << bit) for bit in range(self.bits)] + list(others)
        for target in targets:
            pl.semaphore_signal(barrier, inc=1, device_id=target, device_id_type=MESH)
        pl.semaphore_wait(barrier, len(targets))


def block_of(ref, form, place, shape, half):
    section, dp = place
    if form == "rows":
        rows = shape[-2]
        at = pl.ds(pl.multiple_of(dp * rows, rows), rows)
        return (section, slice(None), at) if len(shape) == 3 else (section, at)
    if form == "columns":
        low, high = half
        return (
            section,
            pl.ds(low, high - low),
            pl.ds(pl.multiple_of(dp * shape[-1], shape[-1]), shape[-1]),
        )
    if len(shape) == 2 and half is not None:
        return (section, dp, pl.ds(half[0], half[1] - half[0]))
    return (section, dp)


def weights_kernel(pieces, count, dp_count, *refs):
    own = refs[:count]
    full = refs[count : 2 * count]
    send_sem, recv_sem, local_sem = refs[2 * count :]
    cube = Cube(dp_count)
    cube.greet()

    def source(piece):
        which, form, shape, half, kind = piece
        return own[which] if half is None else own[which].at[pl.ds(half[0], half[1] - half[0])]

    def slot(piece, mask):
        which, form, shape, half, kind = piece
        return full[which].at[block_of(full[which], form, cube.place(mask), shape, half)]

    def copy_of(number, piece, mask, bit, receiving=False):
        held = mask if receiving else mask ^ (1 << bit)
        return pltpu.make_async_remote_copy(
            src_ref=source(piece) if held == 0 else slot(piece, held),
            dst_ref=slot(piece, held),
            send_sem=send_sem.at[number, mask],
            recv_sem=recv_sem.at[number, mask],
            device_id=cube.device(1 << bit),
            device_id_type=MESH,
        )

    def steps(piece):
        order = cube.order(piece[4])
        held = [0]
        out = []
        for bit in order:
            fresh = [mask | (1 << bit) for mask in held]
            out += [(mask, bit) for mask in fresh]
            held = held + fresh
        return out

    locals_ = []
    for number, piece in enumerate(pieces):
        for mask, bit in steps(piece):
            if mask == 1 << bit:
                copy_of(number, piece, mask, bit).start()
    for number, piece in enumerate(pieces):
        copy = pltpu.make_async_copy(source(piece), slot(piece, 0), local_sem.at[number])
        copy.start()
        locals_.append(copy)
    rounds = cube.size
    waited = [set() for _ in pieces]
    for turn in range(rounds):
        for number, piece in enumerate(pieces):
            relays = [(m, b) for m, b in steps(piece)]
            landing = [m for m, b in relays]
            if turn >= len(landing):
                continue
            mask = landing[turn]
            bit_in = dict(relays)[mask]
            copy_of(number, piece, mask, bit_in, True).wait_recv()
            for later, bit in relays:
                if later ^ (1 << bit) == mask and later != 1 << bit:
                    copy_of(number, piece, later, bit).start()
    for number, piece in enumerate(pieces):
        for mask, bit in steps(piece):
            copy_of(number, piece, mask, bit).wait_send()
    for copy in locals_:
        copy.wait()


def full_shape(form, shape, dp_count):
    if form == "rows":
        return (2,) + shape[:-2] + (dp_count * shape[-2], shape[-1])
    if form == "columns":
        return (2, shape[0], dp_count * shape[1])
    return (2, dp_count) + shape


def pieces_of(forms, shapes):
    pieces = []
    for which, (form, shape) in enumerate(zip(forms, shapes)):
        if which == 3:
            middle = shape[0] // 2
            pieces.append((which, form, shape, (0, middle), 0))
            pieces.append((which, form, shape, (middle, shape[0]), 1))
        elif which == 1:
            pieces.append((which, form, shape, (0, shape[0]), 0))
        else:
            pieces.append((which, form, shape, None, 1 if which == 2 else 0))
    return pieces


def gather_weights(arrays, forms):
    dp_count = lax.axis_size("dp")
    shapes = [array.shape for array in arrays]
    pieces = pieces_of(forms, shapes)
    count = len(arrays)
    return pl.pallas_call(
        functools.partial(weights_kernel, pieces, count, dp_count),
        out_shape=[
            jax.ShapeDtypeStruct(full_shape(form, shape, dp_count), BF16)
            for form, shape in zip(forms, shapes)
        ],
        in_specs=[VMEM_SPEC] * count,
        out_specs=[VMEM_SPEC] * count,
        scratch_shapes=[
            pltpu.SemaphoreType.DMA((len(pieces), 2 * dp_count)),
            pltpu.SemaphoreType.DMA((len(pieces), 2 * dp_count)),
            pltpu.SemaphoreType.DMA((len(pieces),)),
        ],
        compiler_params=pltpu.CompilerParams(
            collective_id=3, has_side_effects=True, vmem_limit_bytes=VMEM_LIMIT
        ),
        name="gather_weights",
    )(*arrays)


def piece_shape(piece):
    which, form, shape, half, kind = piece
    return shape if half is None else (half[1] - half[0],) + shape[1:]


def grads_kernel(pieces, count, dp_count, line, *refs):
    parts = refs[:count]
    sums = refs[count : 2 * count]
    row_sum = refs[2 * count]
    landed = refs[2 * count + 1 : 2 * count + 1 + len(pieces)]
    line_buf, send_sem, recv_sem, line_send, line_recv = refs[2 * count + 1 + len(pieces) :]
    cube = Cube(dp_count)
    here = lax.axis_index("tensor")
    others = [{"tensor": lax.rem(here + step, line)} for step in range(1, line)]
    cube.greet(others)

    def part(piece, mask):
        which, form, shape, half, kind = piece
        return parts[which].at[block_of(parts[which], form, cube.place(mask), shape, half)]

    def plan(piece):
        order = cube.order(piece[4])[::-1]
        active = list(range(cube.size))
        levels = []
        at = 0
        for bit in order:
            kept = [mask for mask in active if not mask & (1 << bit)]
            kept.sort(key=lambda mask: -sum(1 << order.index(b) for b in order if mask & (1 << b)))
            kept.sort(
                key=lambda mask: min(
                    [order.index(b) for b in order if mask & (1 << b)] + [len(order)]
                )
            )
            levels.append((bit, [(mask, at + i) for i, mask in enumerate(kept)]))
            at += len(kept)
            active = kept
        return levels

    plans = [plan(piece) for piece in pieces]

    def slot_of(number, level, mask):
        return dict(plans[number][level][1])[mask]

    def copy_of(number, level, mask):
        piece = pieces[number]
        bit = plans[number][level][0]
        slot = slot_of(number, level, mask)
        sent = mask | (1 << bit)
        return pltpu.make_async_remote_copy(
            src_ref=part(piece, sent)
            if level == 0
            else landed[number].at[slot_of(number, level - 1, sent)],
            dst_ref=landed[number].at[slot],
            send_sem=send_sem.at[number, slot],
            recv_sem=recv_sem.at[number, slot],
            device_id=cube.device(1 << bit),
            device_id_type=MESH,
        )

    for place in range(cube.size // 2):
        for number in range(len(pieces)):
            copy_of(number, 0, plans[number][0][1][place][0]).start()

    def fold(number, level, mask, final):
        piece = pieces[number]
        which, form, shape, half, kind = piece
        slot = slot_of(number, level, mask)
        full = piece_shape(piece)
        rows = full[-2]
        chunk = rows if rows <= 32 else 32
        base = (
            part(piece, mask)
            if level == 0
            else landed[number].at[slot_of(number, level - 1, mask)]
        )
        lead = (slice(None),) * (len(full) - 2)

        def one(index, carry):
            at = pl.ds(pl.multiple_of(index * chunk, chunk), chunk)
            total = base[lead + (at,)].astype(F32) + landed[number][(slot,) + lead + (at,)].astype(F32)
            if final:
                low = 0 if half is None else half[0]
                to = pl.ds(pl.multiple_of(low + index * chunk, chunk), chunk)
                sums[which][lead + (to,)] = total
            else:
                landed[number][(slot,) + lead + (at,)] = total.astype(landed[number].dtype)
            return carry

        if rows == chunk:
            one(0, 0)
        else:
            lax.fori_loop(0, rows // chunk, one, 0)

    depth = cube.bits
    for level in range(depth):
        masks = len(plans[0][level][1])
        for place in range(masks):
            for number in list(range(len(pieces)))[::-1]:
                mask = plans[number][level][1][place][0]
                copy_of(number, level, mask).wait_recv()
                final = level == depth - 1
                fold(number, level, mask, final)
                if not final:
                    bit_next = plans[number][level + 1][0]
                    if mask & (1 << bit_next):
                        copy_of(number, level + 1, mask ^ (1 << bit_next)).start()
                elif pieces[number][0] == count - 1:
                    for step in range(1, line):
                        line_copy(step, others, sums[count - 1], line_buf, line_send, line_recv).start()
    total = sums[count - 1][...]
    for step in range(1, line):
        line_copy(step, others, sums[count - 1], line_buf, line_send, line_recv).wait_recv()
        total = total + line_buf[step - 1]
    row_sum[...] = total
    for step in range(1, line):
        line_copy(step, others, sums[count - 1], line_buf, line_send, line_recv).wait_send()
    for number in range(len(pieces)):
        for level in range(depth):
            for mask, slot in plans[number][level][1]:
                copy_of(number, level, mask).wait_send()


def line_copy(step, others, source, line_buf, line_send, line_recv):
    return pltpu.make_async_remote_copy(
        src_ref=source,
        dst_ref=line_buf.at[step - 1],
        send_sem=line_send.at[step - 1],
        recv_sem=line_recv.at[step - 1],
        device_id=others[step - 1],
        device_id_type=MESH,
    )


def scatter_grads(arrays, forms, shapes):
    dp_count = lax.axis_size("dp")
    line = lax.axis_size("tensor")
    pieces = pieces_of(forms, shapes)
    count = len(arrays)
    slots = 2 * dp_count - 1
    return pl.pallas_call(
        functools.partial(grads_kernel, pieces, count, dp_count, line),
        out_shape=[jax.ShapeDtypeStruct(shape, F32) for shape in shapes]
        + [jax.ShapeDtypeStruct(shapes[-1], F32)],
        in_specs=[VMEM_SPEC] * count,
        out_specs=[VMEM_SPEC] * (count + 1),
        scratch_shapes=[
            pltpu.VMEM((slots,) + piece_shape(piece), arrays[piece[0]].dtype) for piece in pieces
        ]
        + [
            pltpu.VMEM((line - 1,) + shapes[-1], F32),
            pltpu.SemaphoreType.DMA((len(pieces), slots)),
            pltpu.SemaphoreType.DMA((len(pieces), slots)),
            pltpu.SemaphoreType.DMA((line - 1,)),
            pltpu.SemaphoreType.DMA((line - 1,)),
        ],
        compiler_params=pltpu.CompilerParams(
            collective_id=4, has_side_effects=True, vmem_limit_bytes=VMEM_LIMIT
        ),
        name="scatter_grads",
    )(*arrays)


def gelu_exact(values):
    return 0.5 * values * (1.0 + jax.scipy.special.erf(values * 0.7071067811865476))


def gelu_slope(values):
    return (
        0.5 * (1.0 + jax.scipy.special.erf(values * 0.7071067811865476))
        + values * jnp.exp(-0.5 * values * values) * 0.3989422804014327
    )


def normalize(summed):
    center = summed - jnp.mean(summed, axis=-1, keepdims=True)
    scaled = lax.rsqrt(jnp.mean(center * center, axis=-1, keepdims=True) + 1e-12)
    return (center * scaled, scaled)


def norm_back(upstream, normed, scaled):
    return scaled * (
        upstream
        - jnp.mean(upstream, axis=-1, keepdims=True)
        - normed * jnp.mean(upstream * normed, axis=-1, keepdims=True)
    )


def masked_probs(queries, keys, same_seq):
    scores = jnp.einsum(
        "qhd,khd->hqk", queries, keys, preferred_element_type=jnp.float32
    ) * queries.shape[2] ** (-0.5)
    scores = jnp.where(same_seq[None], scores, -jnp.inf)
    largest = jnp.max(scores, axis=-1, keepdims=True)
    shifted = jnp.exp(scores - largest)
    return shifted / jnp.sum(shifted, axis=-1, keepdims=True)


def split_heads(qkv_held, which, head_count, head_size):
    return qkv_held[:, which].reshape(qkv_held.shape[0], head_count, head_size)


def layer_forward(local_rows, pack_ids, weights):
    qkv_mat, qv_shift, out_mat, up_mat, up_shift, down_mat, row_params = weights
    gathered = tensor_gather(local_rows)
    tokens = gathered.shape[0]
    width = qkv_mat.shape[2]
    head_count = qv_shift.shape[1]
    head_size = qv_shift.shape[2]
    projected = jnp.einsum("tc,jcn->tjn", gathered, qkv_mat, preferred_element_type=jnp.float32)
    qv_wide = qv_shift.astype(jnp.float32).reshape(2, width)
    bias_rows = jnp.concatenate(
        [qv_wide[0:1], jnp.zeros((1, width), jnp.float32), qv_wide[1:2]], axis=0
    )
    qkv_held = (projected + bias_rows[None]).astype(jnp.bfloat16)
    queries = split_heads(qkv_held, 0, head_count, head_size)
    keys = split_heads(qkv_held, 1, head_count, head_size)
    values = split_heads(qkv_held, 2, head_count, head_size)
    same_seq = pack_ids[:, None] == pack_ids[None, :]
    attn_prob = masked_probs(queries, keys, same_seq)
    context = (
        jnp.einsum(
            "hqk,khd->qhd",
            attn_prob.astype(jnp.bfloat16),
            values,
            preferred_element_type=jnp.float32,
        )
        .reshape(tokens, width)
        .astype(jnp.bfloat16)
    )
    params_wide = row_params.astype(jnp.float32)
    attn_part = tensor_scatter(jnp.dot(context, out_mat, preferred_element_type=jnp.float32).astype(jnp.bfloat16))
    resid_one = local_rows.astype(jnp.float32) + attn_part + params_wide[0]
    normed_one, scaled_one = normalize(resid_one)
    hidden_one = normed_one * params_wide[1] + params_wide[2]
    hidden_in = tensor_gather(hidden_one.astype(jnp.bfloat16))
    pre_act = jnp.dot(hidden_in, up_mat, preferred_element_type=jnp.float32) + up_shift.astype(
        jnp.float32
    ).reshape(-1)
    activated = gelu_exact(pre_act).astype(jnp.bfloat16)
    resid_two = (
        hidden_one
        + tensor_scatter(jnp.dot(activated, down_mat, preferred_element_type=jnp.float32).astype(jnp.bfloat16))
        + params_wide[3]
    )
    normed_two, scaled_two = normalize(resid_two)
    layer_out = (normed_two * params_wide[4] + params_wide[5]).astype(jnp.bfloat16)
    saved = (
        gathered,
        qkv_held,
        context,
        normed_one,
        scaled_one,
        hidden_in,
        pre_act,
        activated,
        normed_two,
        scaled_two,
    )
    return (layer_out, saved)


def layer_backward(upstream, pack_ids, weights, saved):
    qkv_mat, qv_shift, out_mat, up_mat, up_shift, down_mat, row_params = weights
    (
        gathered,
        qkv_held,
        context,
        normed_one,
        scaled_one,
        hidden_in,
        pre_act,
        activated,
        normed_two,
        scaled_two,
    ) = saved
    tokens = gathered.shape[0]
    width = qkv_mat.shape[2]
    head_count = qv_shift.shape[1]
    head_size = qv_shift.shape[2]
    params_wide = row_params.astype(jnp.float32)
    grad_two = norm_back(upstream * params_wide[4], normed_two, scaled_two)
    grad_full = tensor_gather(grad_two.astype(jnp.bfloat16))
    down_grad = jnp.dot(activated.T, grad_full, preferred_element_type=jnp.float32)
    grad_pre = jnp.dot(grad_full, down_mat.T, preferred_element_type=jnp.float32) * gelu_slope(
        pre_act
    )
    grad_pre_held = grad_pre.astype(jnp.bfloat16)
    up_grad = jnp.dot(hidden_in.T, grad_pre_held, preferred_element_type=jnp.float32)
    grad_hidden = grad_two + tensor_scatter(jnp.dot(grad_pre_held, up_mat.T, preferred_element_type=jnp.float32).astype(jnp.bfloat16))
    grad_one = norm_back(grad_hidden * params_wide[1], normed_one, scaled_one)
    resid_full = tensor_gather(grad_one.astype(jnp.bfloat16))
    out_grad = jnp.dot(context.T, resid_full, preferred_element_type=jnp.float32)
    grad_context = (
        jnp.dot(resid_full, out_mat.T, preferred_element_type=jnp.float32)
        .astype(jnp.bfloat16)
        .reshape(tokens, head_count, head_size)
    )
    queries = split_heads(qkv_held, 0, head_count, head_size)
    keys = split_heads(qkv_held, 1, head_count, head_size)
    values = split_heads(qkv_held, 2, head_count, head_size)
    same_seq = pack_ids[:, None] == pack_ids[None, :]
    attn_prob = masked_probs(queries, keys, same_seq)
    grad_prob = jnp.einsum("qhd,khd->hqk", grad_context, values, preferred_element_type=jnp.float32)
    row_dots = jnp.sum(attn_prob * grad_prob, axis=-1, keepdims=True)
    grad_scores = (attn_prob * (grad_prob - row_dots) * head_size ** (-0.5)).astype(jnp.bfloat16)
    grad_queries = jnp.einsum("hqk,khd->qhd", grad_scores, keys, preferred_element_type=jnp.float32)
    grad_keys = jnp.einsum("hqk,qhd->khd", grad_scores, queries, preferred_element_type=jnp.float32)
    grad_values = jnp.einsum(
        "hqk,qhd->khd",
        attn_prob.astype(jnp.bfloat16),
        grad_context,
        preferred_element_type=jnp.float32,
    )
    qv_grad = jnp.stack([jnp.sum(grad_queries, axis=0), jnp.sum(grad_values, axis=0)])
    grad_qkv = (
        jnp.stack([grad_queries, grad_keys, grad_values], axis=1)
        .reshape(tokens, 3, width)
        .astype(jnp.bfloat16)
    )
    qkv_grad = jnp.einsum("tc,tjn->jcn", gathered, grad_qkv, preferred_element_type=jnp.float32)
    grad_inputs = grad_one + tensor_scatter(jnp.einsum("tjn,jcn->tc", grad_qkv, qkv_mat, preferred_element_type=jnp.float32).astype(
            jnp.bfloat16
        ))
    row_grads = jnp.stack(
        [
            jnp.sum(grad_one, axis=0),
            jnp.sum(grad_hidden * normed_one, axis=0),
            jnp.sum(grad_hidden, axis=0),
            jnp.sum(grad_two, axis=0),
            jnp.sum(upstream * normed_two, axis=0),
            jnp.sum(upstream, axis=0),
        ]
    )
    up_shift_grad = jnp.sum(grad_pre, axis=0).reshape(up_shift.shape)
    return (
        grad_inputs,
        (qkv_grad, qv_grad, out_grad, up_grad, up_shift_grad, down_grad),
        row_grads,
    )


def shards(
    block_input,
    seq_ids,
    out_cotangent,
    qkv_weight,
    qv_bias,
    out_weight,
    out_bias,
    norm1_gain,
    norm1_bias,
    up_weight,
    up_bias,
    down_weight,
    down_bias,
    norm2_gain,
    norm2_bias,
):
    section = lax.axis_index("section")
    first = section == 0
    dp_count = lax.axis_size("dp")
    line = lax.axis_size("tensor")
    heads, head_part = qv_bias.shape[2], qv_bias.shape[3]
    groups, unit_part = up_bias.shape[1], up_bias.shape[2]
    part = out_bias.shape[1]
    columns = "columns" if part % 128 == 0 else "stack"
    forms = ["rows", columns, "rows", columns, "stack"]

    small_sizes = (qv_bias[0].size, up_bias[0].size, 6 * part)
    small_rows = -(-sum(small_sizes) // 2048) * 16
    small = jnp.concatenate(
        [
            qv_bias.reshape(-1),
            up_bias.reshape(-1),
            out_bias[0],
            norm1_gain[0],
            norm1_bias[0],
            down_bias[0],
            norm2_gain[0],
            norm2_bias[0],
            jnp.zeros((small_rows * 128 - sum(small_sizes),), BF16),
        ]
    ).reshape(small_rows, 128)
    stacked = gather_weights(
        (jnp.swapaxes(qkv_weight[0], 0, 1), out_weight[0], up_weight[0], down_weight[0], small),
        forms,
    )

    def layer_weights(which):
        qkv_full, out_full, up_full, down_full, small_full = [array[which] for array in stacked]
        if columns == "stack":
            out_full, down_full = [
                jnp.moveaxis(array, 0, 1).reshape(array.shape[1], -1)
                for array in (out_full, down_full)
            ]
        flat = small_full.reshape(dp_count, -1)
        qv_full = flat[:, : small_sizes[0]].reshape(dp_count, 2, heads, head_part)
        qv_full = jnp.moveaxis(qv_full, 0, 2).reshape(2, heads, dp_count * head_part)
        middle = small_sizes[0] + small_sizes[1]
        up_shift = flat[:, small_sizes[0] : middle].reshape(dp_count, groups, unit_part)
        up_shift = jnp.moveaxis(up_shift, 0, 1).reshape(groups, dp_count * unit_part)
        row_params = flat[:, middle : middle + small_sizes[2]].reshape(dp_count, 6, part)
        row_params = jnp.moveaxis(row_params, 0, 1).reshape(6, dp_count * part)
        return (qkv_full, qv_full, out_full, up_full, up_shift, down_full, row_params)

    weights = [layer_weights(0), layer_weights(1)]
    rows = jnp.where(first, block_input[0, 0], block_input[1, 0])
    ids = jnp.where(first, seq_ids[0, 0], seq_ids[1, 0])
    upstream = jnp.where(first, out_cotangent[0, 0], out_cotangent[1, 0]).astype(F32)
    out_first, saved_first = layer_forward(rows, ids, weights[0])
    out_last, saved_last = layer_forward(out_first, ids, weights[1])
    swap = [(0, 1), (1, 0)]
    other_out = lax.ppermute(jnp.where(first, out_last, out_first), "section", swap)
    own_out = jnp.where(first, out_first, out_last)
    section_outputs = jnp.stack(
        [jnp.where(first, own_out, other_out), jnp.where(first, other_out, own_out)]
    )
    grad_last, mats_last, rows_last = layer_backward(upstream, ids, weights[1], saved_last)
    grad_first, mats_first, rows_first = layer_backward(grad_last, ids, weights[0], saved_first)
    other_grad = lax.ppermute(
        jnp.where(first, grad_last, grad_first).astype(BF16), "section", swap
    ).astype(F32)
    own_grad = jnp.where(first, grad_first, grad_last)
    input_grads = jnp.stack(
        [jnp.where(first, own_grad, other_grad), jnp.where(first, other_grad, own_grad)]
    )

    def blocks(array):
        cut = array.reshape(array.shape[:-1] + (dp_count, array.shape[-1] // dp_count))
        return jnp.moveaxis(cut, -2, 0)

    def padded(flat):
        size = -(-flat.shape[1] // 1024) * 1024
        return jnp.pad(flat, ((0, 0), (0, size - flat.shape[1]))).reshape(dp_count, -1, 128)

    def packed(mats, row_grads):
        qkv_grad, qv_grad, out_grad, up_grad, up_shift_grad, down_grad = mats
        qv_flat = blocks(qv_grad.reshape(2, heads, -1)).reshape(dp_count, -1)
        up_flat = blocks(up_shift_grad).reshape(dp_count, -1)
        bias_flat = padded(jnp.concatenate([qv_flat, up_flat], axis=1))
        row_flat = padded(blocks(row_grads).reshape(dp_count, -1))
        if columns == "stack":
            out_grad, down_grad = blocks(out_grad), blocks(down_grad)
        return (
            qkv_grad.astype(BF16),
            out_grad.astype(BF16),
            up_grad.astype(BF16),
            down_grad.astype(BF16),
            bias_flat,
            row_flat,
        )

    both = [
        jnp.stack(pair) for pair in zip(packed(mats_first, rows_first), packed(mats_last, rows_last))
    ]
    shapes = [
        (3, part, qkv_weight.shape[3]),
        out_weight.shape[1:],
        up_weight.shape[1:],
        down_weight.shape[1:],
        both[4].shape[2:],
        both[5].shape[2:],
    ]
    qkv_sum, out_sum, up_sum, down_sum, bias_sum, _, row_sum = scatter_grads(
        both, forms + ["stack"], shapes
    )
    bias_sum = bias_sum.reshape(-1)
    qv_sum = bias_sum[: small_sizes[0]].reshape(1, 2, heads, head_part)
    up_shift_sum = bias_sum[small_sizes[0] : small_sizes[0] + small_sizes[1]].reshape(
        1, groups, unit_part
    )
    row_sum = row_sum.reshape(-1)[: 6 * part].reshape(6, line, part // line)
    row_sum = lax.dynamic_index_in_dim(row_sum, lax.axis_index("tensor"), 1, keepdims=False)
    return (
        section_outputs[None, :, None],
        input_grads[None, :, None],
        jnp.swapaxes(qkv_sum, 0, 1)[None],
        qv_sum,
        out_sum[None],
        row_sum[0][None],
        row_sum[1][None],
        row_sum[2][None],
        up_sum[None],
        up_shift_sum,
        down_sum[None],
        row_sum[3][None],
        row_sum[4][None],
        row_sum[5][None],
    )


def solution(mesh):
    return jax.shard_map(
        shards,
        mesh=mesh,
        in_specs=(
            P(None, "dp", "tensor", None),
            P(None, "dp", None),
            P(None, "dp", "tensor", None),
            P("section", "dp", None, "tensor"),
            P("section", None, "tensor", "dp"),
            P("section", "tensor", "dp"),
            P("section", "dp"),
            P("section", "dp"),
            P("section", "dp"),
            P("section", "dp", "tensor"),
            P("section", "tensor", "dp"),
            P("section", "tensor", "dp"),
            P("section", "dp"),
            P("section", "dp"),
            P("section", "dp"),
        ),
        out_specs=(
            P("section", None, "dp", "tensor", None),
            P("section", None, "dp", "tensor", None),
            P("section", "dp", None, "tensor"),
            P("section", None, "tensor", "dp"),
            P("section", "tensor", "dp"),
            P("section", ("dp", "tensor")),
            P("section", ("dp", "tensor")),
            P("section", ("dp", "tensor")),
            P("section", "dp", "tensor"),
            P("section", "tensor", "dp"),
            P("section", "tensor", "dp"),
            P("section", ("dp", "tensor")),
            P("section", ("dp", "tensor")),
            P("section", ("dp", "tensor")),
        ),
        check_vma=False,
    )
```

```python
import functools

import jax
import jax.numpy as jnp
from jax import lax
from jax.experimental import pallas as pl
from jax.experimental.pallas import tpu as pltpu
from jax.sharding import PartitionSpec as P

MESH = pl.DeviceIdType.MESH
F32 = jnp.float32
BF16 = jnp.bfloat16
VMEM_SPEC = pl.BlockSpec(memory_space=pltpu.VMEM)
VMEM_LIMIT = 60 * 1024 * 1024


def line_barrier(me, count, others=()):
    barrier = pltpu.get_barrier_semaphore()
    for target in others:
        pl.semaphore_signal(barrier, inc=1, device_id=target, device_id_type=MESH)

    @pl.when(me > 0)
    def _():
        pl.semaphore_signal(barrier, inc=1, device_id={"tensor": me - 1}, device_id_type=MESH)

    @pl.when(me < count - 1)
    def _():
        pl.semaphore_signal(barrier, inc=1, device_id={"tensor": me + 1}, device_id_type=MESH)

    inner = jnp.logical_and(me > 0, me < count - 1)

    @pl.when(inner)
    def _():
        pl.semaphore_wait(barrier, 2 + len(others))

    @pl.when(jnp.logical_not(inner))
    def _():
        pl.semaphore_wait(barrier, 1 + len(others))


def gather_steps(count, own_ref, all_ref, send_sem, recv_sem):
    me = lax.axis_index("tensor")

    def copy_of(side, step):
        shard = me - step if side == 0 else me + step
        target = me + 1 if side == 0 else me - 1
        return pltpu.make_async_remote_copy(
            src_ref=own_ref if step == 0 else all_ref.at[shard],
            dst_ref=all_ref.at[shard],
            send_sem=send_sem.at[side, step],
            recv_sem=recv_sem.at[side, step],
            device_id={"tensor": target},
            device_id_type=MESH,
        )

    def arrival(side, step):
        shard = me - step if side == 0 else me + step
        return pltpu.make_async_remote_copy(
            src_ref=all_ref.at[shard],
            dst_ref=all_ref.at[shard],
            send_sem=send_sem.at[side, step - 1],
            recv_sem=recv_sem.at[side, step - 1],
            device_id={"tensor": me - 1 if side == 0 else me + 1},
            device_id_type=MESH,
        )

    def holds(side, step):
        return me >= step if side == 0 else me + step <= count - 1

    def sends(side):
        return me < count - 1 if side == 0 else me > 0

    for step in range(count):
        for side in range(2):

            @pl.when(holds(side, step))
            def _():
                if step > 0:
                    arrival(side, step).wait_recv()
                if step < count - 1:

                    @pl.when(sends(side))
                    def _():
                        copy_of(side, step).start()

        if step == 0:
            all_ref[me] = own_ref[...]
        yield
    for step in range(count - 1):
        for side in range(2):

            @pl.when(holds(side, step))
            def _():
                @pl.when(sends(side))
                def _():
                    copy_of(side, step).wait_send()


def gather_kernel(count, own_ref, all_ref, send_sem, recv_sem):
    line_barrier(lax.axis_index("tensor"), count)
    for _ in gather_steps(count, own_ref, all_ref, send_sem, recv_sem):
        pass


def tensor_gather(rows):
    count = lax.axis_size("tensor")
    gathered = pl.pallas_call(
        functools.partial(gather_kernel, count),
        out_shape=jax.ShapeDtypeStruct((count,) + rows.shape, rows.dtype),
        in_specs=[VMEM_SPEC],
        out_specs=VMEM_SPEC,
        scratch_shapes=[
            pltpu.SemaphoreType.DMA((2, count - 1)),
            pltpu.SemaphoreType.DMA((2, count - 1)),
        ],
        compiler_params=pltpu.CompilerParams(collective_id=1, has_side_effects=True),
        name="tensor_gather",
    )(rows)
    return gathered.reshape(count * rows.shape[0], rows.shape[1])


def scatter_steps(count, part_ref, sum_ref, landed, staged, send_sem, recv_sem):
    me = lax.axis_index("tensor")

    def copy_of(side, slot, first, dest):
        return pltpu.make_async_remote_copy(
            src_ref=part_ref.at[dest] if first else staged.at[side, slot],
            dst_ref=landed.at[side, slot],
            send_sem=send_sem.at[side, slot],
            recv_sem=recv_sem.at[side, slot],
            device_id={"tensor": me + 1 if side == 0 else me - 1},
            device_id_type=MESH,
        )

    def roles(side, slot):
        dest = count - 1 - slot if side == 0 else slot
        passes = me < dest if side == 0 else me > dest
        first = me == 0 if side == 0 else me == count - 1
        return dest, passes, first

    for slot in range(count - 1):
        for side in range(2):
            dest, passes, first = roles(side, slot)

            @pl.when(first)
            def _():
                copy_of(side, slot, True, dest).start()

    yield
    for slot in range(count - 1):
        for side in range(2):
            dest, passes, first = roles(side, slot)

            @pl.when(jnp.logical_and(passes, jnp.logical_not(first)))
            def _():
                copy_of(side, slot, False, dest).wait_recv()
                staged[side, slot] = (
                    part_ref[dest].astype(F32) + landed[side, slot].astype(F32)
                ).astype(BF16)
                copy_of(side, slot, False, dest).start()

        yield
    for place in range(count):

        @pl.when(me == place)
        def _():
            total = part_ref[place].astype(F32)
            if place > 0:
                copy_of(0, count - 1 - place, False, place).wait_recv()
                total = total + landed[0, count - 1 - place].astype(F32)
            if place < count - 1:
                copy_of(1, place, False, place).wait_recv()
                total = total + landed[1, place].astype(F32)
            sum_ref[...] = total

    for slot in range(count - 1):
        for side in range(2):
            dest, passes, first = roles(side, slot)

            @pl.when(passes)
            def _():
                copy_of(side, slot, False, dest).wait_send()


def scatter_kernel(count, part_ref, sum_ref, landed, staged, send_sem, recv_sem):
    line_barrier(lax.axis_index("tensor"), count)
    for _ in scatter_steps(count, part_ref, sum_ref, landed, staged, send_sem, recv_sem):
        pass


def tensor_scatter(parts):
    count = lax.axis_size("tensor")
    rows = parts.shape[0] // count
    width = parts.shape[1]
    return pl.pallas_call(
        functools.partial(scatter_kernel, count),
        out_shape=jax.ShapeDtypeStruct((rows, width), F32),
        in_specs=[VMEM_SPEC],
        out_specs=VMEM_SPEC,
        scratch_shapes=[
            pltpu.VMEM((2, count - 1, rows, width), BF16),
            pltpu.VMEM((2, count - 1, rows, width), BF16),
            pltpu.SemaphoreType.DMA((2, count - 1)),
            pltpu.SemaphoreType.DMA((2, count - 1)),
        ],
        compiler_params=pltpu.CompilerParams(collective_id=2, has_side_effects=True),
        name="tensor_scatter",
    )(parts.reshape(count, rows, width))


class Cube:
    def __init__(self, dp_count):
        self.dp_count = dp_count
        self.dp_bits = dp_count.bit_length() - 1
        self.bits = self.dp_bits + 1
        self.size = 2 * dp_count
        self.section = lax.axis_index("section")
        self.dp = lax.axis_index("dp")

    def place(self, mask):
        section = 1 - self.section if mask & self.dp_count else self.section
        dp = self.dp
        for bit in range(self.dp_bits):
            if mask & (1 << bit):
                dp = dp + (1 << bit) * (1 - 2 * ((self.dp // (1 << bit)) % 2))
        return section, dp

    def device(self, mask):
        section, dp = self.place(mask)
        return {"section": section, "dp": dp}

    def order(self, kind):
        bits = list(range(self.bits - 1, -1, -1))
        if kind:
            bits[0], bits[1] = bits[1], bits[0]
        return bits

    def greet(self, others=()):
        barrier = pltpu.get_barrier_semaphore()
        targets = [self.device(1 << bit) for bit in range(self.bits)] + list(others)
        for target in targets:
            pl.semaphore_signal(barrier, inc=1, device_id=target, device_id_type=MESH)
        pl.semaphore_wait(barrier, len(targets))


def block_of(ref, form, place, shape, half):
    section, dp = place
    if form == "rows":
        rows = shape[-2]
        low, high = half or (0, rows)
        at = pl.ds(pl.multiple_of(dp * rows + low, high - low), high - low)
        return (section, slice(None), at) if len(shape) == 3 else (section, at)
    if form == "columns":
        low, high = half
        return (
            section,
            pl.ds(low, high - low),
            pl.ds(pl.multiple_of(dp * shape[-1], shape[-1]), shape[-1]),
        )
    if len(shape) == 2 and half is not None:
        return (section, dp, pl.ds(half[0], half[1] - half[0]))
    return (section, dp)


def weights_steps(pieces, cube, own, full, send_sem, recv_sem, local_sem):

    def source(piece):
        which, form, shape, half, kind = piece
        return own[which] if half is None else own[which].at[pl.ds(half[0], half[1] - half[0])]

    def slot(piece, mask):
        which, form, shape, half, kind = piece
        return full[which].at[block_of(full[which], form, cube.place(mask), shape, half)]

    def copy_of(number, piece, mask, bit, receiving=False):
        held = mask if receiving else mask ^ (1 << bit)
        return pltpu.make_async_remote_copy(
            src_ref=source(piece) if held == 0 else slot(piece, held),
            dst_ref=slot(piece, held),
            send_sem=send_sem.at[number, mask],
            recv_sem=recv_sem.at[number, mask],
            device_id=cube.device(1 << bit),
            device_id_type=MESH,
        )

    def steps(piece):
        order = cube.order(piece[4])
        held = [0]
        out = []
        for bit in order:
            fresh = [mask | (1 << bit) for mask in held]
            out += [(mask, bit) for mask in fresh]
            held = held + fresh
        return out

    locals_ = []
    for number, piece in enumerate(pieces):
        for mask, bit in steps(piece):
            if mask == 1 << bit:
                copy_of(number, piece, mask, bit).start()
    for number, piece in enumerate(pieces):
        copy = pltpu.make_async_copy(source(piece), slot(piece, 0), local_sem.at[number])
        copy.start()
        locals_.append(copy)
    yield
    for turn in range(cube.size - 1):
        for number, piece in enumerate(pieces):
            relays = [(m, b) for m, b in steps(piece)]
            landing = [m for m, b in relays]
            if turn >= len(landing):
                continue
            mask = landing[turn]
            bit_in = dict(relays)[mask]
            copy_of(number, piece, mask, bit_in, True).wait_recv()
            for later, bit in relays:
                if later ^ (1 << bit) == mask and later != 1 << bit:
                    copy_of(number, piece, later, bit).start()
        yield
    for number, piece in enumerate(pieces):
        for mask, bit in steps(piece):
            copy_of(number, piece, mask, bit).wait_send()
    for copy in locals_:
        copy.wait()


def full_shape(form, shape, dp_count):
    if form == "rows":
        return (2,) + shape[:-2] + (dp_count * shape[-2], shape[-1])
    if form == "columns":
        return (2, shape[0], dp_count * shape[1])
    return (2, dp_count) + shape


def pieces_of(forms, shapes):
    pieces = []
    for which, (form, shape) in enumerate(zip(forms, shapes)):
        if which == 3:
            middle = shape[0] // 2
            pieces.append((which, form, shape, (0, middle), 0))
            pieces.append((which, form, shape, (middle, shape[0]), 1))
        elif which == 1:
            pieces.append((which, form, shape, (0, shape[0]), 0))
        else:
            pieces.append((which, form, shape, None, 1 if which == 2 else 0))
    return pieces


def halves_of(forms, shapes):
    pieces = []
    for which, (form, shape) in enumerate(zip(forms, shapes)):
        if len(shape) == 2 and shape[0] >= 64:
            middle = shape[0] // 2
            first = 1 if len(shapes) > 1 else 0
            pieces.append((which, form, shape, (0, middle), first))
            pieces.append((which, form, shape, (middle, shape[0]), 1))
        else:
            pieces.append((which, form, shape, None, 0))
    return pieces


def joint_kernel(scatters, line, pieces, count, dp_count, *refs):
    cube = Cube(dp_count)
    line_barrier(
        lax.axis_index("tensor"), line, [cube.device(1 << bit) for bit in range(cube.bits)]
    )
    rows, own = refs[0], refs[1 : 1 + count]
    result, full = refs[1 + count], refs[2 + count : 2 + 2 * count]
    rest = refs[2 + 2 * count :]
    steps = scatter_steps if scatters else gather_steps
    tensor = steps(line, rows, result, *rest[3:])
    weights = weights_steps(pieces, cube, own, full, *rest[:3])
    running = [tensor, weights]
    while running:
        for one in list(running):
            if next(one, "end") == "end":
                running.remove(one)


def joint_link(number, rows, arrays, forms):
    line = lax.axis_size("tensor")
    dp_count = lax.axis_size("dp")
    scatters = number % 2 == 1
    shapes = [array.shape for array in arrays]
    pieces = halves_of(forms, shapes)
    count = len(arrays)
    depth, width = rows.shape
    line_sems = [pltpu.SemaphoreType.DMA((2, line - 1)), pltpu.SemaphoreType.DMA((2, line - 1))]
    if scatters:
        depth = depth // line
        rows = rows.reshape(line, depth, width)
        result = jax.ShapeDtypeStruct((depth, width), F32)
        line_scratch = [pltpu.VMEM((2, line - 1, depth, width), BF16)] * 2 + line_sems
    else:
        result = jax.ShapeDtypeStruct((line, depth, width), rows.dtype)
        line_scratch = line_sems
    results = pl.pallas_call(
        functools.partial(joint_kernel, scatters, line, pieces, count, dp_count),
        out_shape=[result]
        + [
            jax.ShapeDtypeStruct(full_shape(form, shape, dp_count), BF16)
            for form, shape in zip(forms, shapes)
        ],
        in_specs=[VMEM_SPEC] * (1 + count),
        out_specs=[VMEM_SPEC] * (1 + count),
        scratch_shapes=[
            pltpu.SemaphoreType.DMA((len(pieces), 2 * dp_count)),
            pltpu.SemaphoreType.DMA((len(pieces), 2 * dp_count)),
            pltpu.SemaphoreType.DMA((len(pieces),)),
        ]
        + line_scratch,
        compiler_params=pltpu.CompilerParams(
            collective_id=5 + number, has_side_effects=True, vmem_limit_bytes=VMEM_LIMIT
        ),
        name="joint_link",
    )(rows, *arrays)
    if scatters:
        return results[0], results[1:]
    return results[0].reshape(line * depth, width), results[1:]


def piece_shape(piece):
    which, form, shape, half, kind = piece
    return shape if half is None else (half[1] - half[0],) + shape[1:]


def grads_kernel(pieces, count, dp_count, line, *refs):
    parts = refs[:count]
    sums = refs[count : 2 * count]
    row_sum = refs[2 * count]
    landed = refs[2 * count + 1 : 2 * count + 1 + len(pieces)]
    line_buf, send_sem, recv_sem, line_send, line_recv = refs[2 * count + 1 + len(pieces) :]
    cube = Cube(dp_count)
    here = lax.axis_index("tensor")
    others = [{"tensor": lax.rem(here + step, line)} for step in range(1, line)]
    cube.greet(others)

    def part(piece, mask):
        which, form, shape, half, kind = piece
        return parts[which].at[block_of(parts[which], form, cube.place(mask), shape, half)]

    def plan(piece):
        order = cube.order(piece[4])[::-1]
        active = list(range(cube.size))
        levels = []
        at = 0
        for bit in order:
            kept = [mask for mask in active if not mask & (1 << bit)]
            kept.sort(key=lambda mask: -sum(1 << order.index(b) for b in order if mask & (1 << b)))
            kept.sort(
                key=lambda mask: min(
                    [order.index(b) for b in order if mask & (1 << b)] + [len(order)]
                )
            )
            levels.append((bit, [(mask, at + i) for i, mask in enumerate(kept)]))
            at += len(kept)
            active = kept
        return levels

    plans = [plan(piece) for piece in pieces]

    def slot_of(number, level, mask):
        return dict(plans[number][level][1])[mask]

    def copy_of(number, level, mask):
        piece = pieces[number]
        bit = plans[number][level][0]
        slot = slot_of(number, level, mask)
        sent = mask | (1 << bit)
        return pltpu.make_async_remote_copy(
            src_ref=part(piece, sent)
            if level == 0
            else landed[number].at[slot_of(number, level - 1, sent)],
            dst_ref=landed[number].at[slot],
            send_sem=send_sem.at[number, slot],
            recv_sem=recv_sem.at[number, slot],
            device_id=cube.device(1 << bit),
            device_id_type=MESH,
        )

    for place in range(cube.size // 2):
        for number in range(len(pieces)):
            copy_of(number, 0, plans[number][0][1][place][0]).start()

    def fold(number, level, mask, final):
        piece = pieces[number]
        which, form, shape, half, kind = piece
        slot = slot_of(number, level, mask)
        full = piece_shape(piece)
        rows = full[-2]
        chunk = rows if rows <= 32 else 32
        base = (
            part(piece, mask)
            if level == 0
            else landed[number].at[slot_of(number, level - 1, mask)]
        )
        lead = (slice(None),) * (len(full) - 2)

        def one(index, carry):
            at = pl.ds(pl.multiple_of(index * chunk, chunk), chunk)
            total = base[lead + (at,)].astype(F32) + landed[number][(slot,) + lead + (at,)].astype(F32)
            if final:
                low = 0 if half is None else half[0]
                to = pl.ds(pl.multiple_of(low + index * chunk, chunk), chunk)
                sums[which][lead + (to,)] = total
            else:
                landed[number][(slot,) + lead + (at,)] = total.astype(landed[number].dtype)
            return carry

        if rows == chunk:
            one(0, 0)
        else:
            lax.fori_loop(0, rows // chunk, one, 0)

    depth = cube.bits
    for level in range(depth):
        masks = len(plans[0][level][1])
        for place in range(masks):
            for number in list(range(len(pieces)))[::-1]:
                mask = plans[number][level][1][place][0]
                copy_of(number, level, mask).wait_recv()
                final = level == depth - 1
                fold(number, level, mask, final)
                if not final:
                    bit_next = plans[number][level + 1][0]
                    if mask & (1 << bit_next):
                        copy_of(number, level + 1, mask ^ (1 << bit_next)).start()
                elif pieces[number][0] == count - 1:
                    for step in range(1, line):
                        line_copy(step, others, sums[count - 1], line_buf, line_send, line_recv).start()
    total = sums[count - 1][...]
    for step in range(1, line):
        line_copy(step, others, sums[count - 1], line_buf, line_send, line_recv).wait_recv()
        total = total + line_buf[step - 1]
    row_sum[...] = total
    for step in range(1, line):
        line_copy(step, others, sums[count - 1], line_buf, line_send, line_recv).wait_send()
    for number in range(len(pieces)):
        for level in range(depth):
            for mask, slot in plans[number][level][1]:
                copy_of(number, level, mask).wait_send()


def line_copy(step, others, source, line_buf, line_send, line_recv):
    return pltpu.make_async_remote_copy(
        src_ref=source,
        dst_ref=line_buf.at[step - 1],
        send_sem=line_send.at[step - 1],
        recv_sem=line_recv.at[step - 1],
        device_id=others[step - 1],
        device_id_type=MESH,
    )


def scatter_grads(arrays, forms, shapes):
    dp_count = lax.axis_size("dp")
    line = lax.axis_size("tensor")
    pieces = pieces_of(forms, shapes)
    count = len(arrays)
    slots = 2 * dp_count - 1
    return pl.pallas_call(
        functools.partial(grads_kernel, pieces, count, dp_count, line),
        out_shape=[jax.ShapeDtypeStruct(shape, F32) for shape in shapes]
        + [jax.ShapeDtypeStruct(shapes[-1], F32)],
        in_specs=[VMEM_SPEC] * count,
        out_specs=[VMEM_SPEC] * (count + 1),
        scratch_shapes=[
            pltpu.VMEM((slots,) + piece_shape(piece), arrays[piece[0]].dtype) for piece in pieces
        ]
        + [
            pltpu.VMEM((line - 1,) + shapes[-1], F32),
            pltpu.SemaphoreType.DMA((len(pieces), slots)),
            pltpu.SemaphoreType.DMA((len(pieces), slots)),
            pltpu.SemaphoreType.DMA((line - 1,)),
            pltpu.SemaphoreType.DMA((line - 1,)),
        ],
        compiler_params=pltpu.CompilerParams(
            collective_id=4, has_side_effects=True, vmem_limit_bytes=VMEM_LIMIT
        ),
        name="scatter_grads",
    )(*arrays)


def gelu_exact(values):
    return 0.5 * values * (1.0 + jax.scipy.special.erf(values * 0.7071067811865476))


def gelu_slope(values):
    return (
        0.5 * (1.0 + jax.scipy.special.erf(values * 0.7071067811865476))
        + values * jnp.exp(-0.5 * values * values) * 0.3989422804014327
    )


def normalize(summed):
    center = summed - jnp.mean(summed, axis=-1, keepdims=True)
    scaled = lax.rsqrt(jnp.mean(center * center, axis=-1, keepdims=True) + 1e-12)
    return (center * scaled, scaled)


def norm_back(upstream, normed, scaled):
    return scaled * (
        upstream
        - jnp.mean(upstream, axis=-1, keepdims=True)
        - normed * jnp.mean(upstream * normed, axis=-1, keepdims=True)
    )


def masked_probs(queries, keys, same_seq):
    scores = jnp.einsum(
        "qhd,khd->hqk", queries, keys, preferred_element_type=jnp.float32
    ) * queries.shape[2] ** (-0.5)
    scores = jnp.where(same_seq[None], scores, -jnp.inf)
    largest = jnp.max(scores, axis=-1, keepdims=True)
    shifted = jnp.exp(scores - largest)
    return shifted / jnp.sum(shifted, axis=-1, keepdims=True)


def split_heads(qkv_held, which, head_count, head_size):
    return qkv_held[:, which].reshape(qkv_held.shape[0], head_count, head_size)


def layer_forward(local_rows, pack_ids, link, weights):
    gathered = link(0, local_rows)
    qkv_mat, qv_shift, out_mat, up_shift, row_params = weights(0)
    tokens = gathered.shape[0]
    width = qkv_mat.shape[2]
    head_count = qv_shift.shape[1]
    head_size = qv_shift.shape[2]
    projected = jnp.einsum("tc,jcn->tjn", gathered, qkv_mat, preferred_element_type=jnp.float32)
    qv_wide = qv_shift.astype(jnp.float32).reshape(2, width)
    bias_rows = jnp.concatenate(
        [qv_wide[0:1], jnp.zeros((1, width), jnp.float32), qv_wide[1:2]], axis=0
    )
    qkv_held = (projected + bias_rows[None]).astype(jnp.bfloat16)
    queries = split_heads(qkv_held, 0, head_count, head_size)
    keys = split_heads(qkv_held, 1, head_count, head_size)
    values = split_heads(qkv_held, 2, head_count, head_size)
    same_seq = pack_ids[:, None] == pack_ids[None, :]
    attn_prob = masked_probs(queries, keys, same_seq)
    context = (
        jnp.einsum(
            "hqk,khd->qhd",
            attn_prob.astype(jnp.bfloat16),
            values,
            preferred_element_type=jnp.float32,
        )
        .reshape(tokens, width)
        .astype(jnp.bfloat16)
    )
    params_wide = row_params.astype(jnp.float32)
    attn_part = link(1, jnp.dot(context, out_mat, preferred_element_type=jnp.float32).astype(jnp.bfloat16))
    resid_one = local_rows.astype(jnp.float32) + attn_part + params_wide[0]
    normed_one, scaled_one = normalize(resid_one)
    hidden_one = normed_one * params_wide[1] + params_wide[2]
    up_mat = weights(1)
    hidden_in = link(2, hidden_one.astype(jnp.bfloat16))
    down_mat = weights(2)
    pre_act = jnp.dot(hidden_in, up_mat, preferred_element_type=jnp.float32) + up_shift.astype(
        jnp.float32
    ).reshape(-1)
    activated = gelu_exact(pre_act).astype(jnp.bfloat16)
    resid_two = (
        hidden_one
        + link(3, jnp.dot(activated, down_mat, preferred_element_type=jnp.float32).astype(jnp.bfloat16))
        + params_wide[3]
    )
    normed_two, scaled_two = normalize(resid_two)
    layer_out = (normed_two * params_wide[4] + params_wide[5]).astype(jnp.bfloat16)
    saved = (
        gathered,
        qkv_held,
        context,
        normed_one,
        scaled_one,
        hidden_in,
        pre_act,
        activated,
        normed_two,
        scaled_two,
    )
    return (layer_out, saved)


def layer_backward(upstream, pack_ids, weights, saved):
    qkv_mat, qv_shift, out_mat, up_mat, up_shift, down_mat, row_params = weights
    (
        gathered,
        qkv_held,
        context,
        normed_one,
        scaled_one,
        hidden_in,
        pre_act,
        activated,
        normed_two,
        scaled_two,
    ) = saved
    tokens = gathered.shape[0]
    width = qkv_mat.shape[2]
    head_count = qv_shift.shape[1]
    head_size = qv_shift.shape[2]
    params_wide = row_params.astype(jnp.float32)
    grad_two = norm_back(upstream * params_wide[4], normed_two, scaled_two)
    grad_full = tensor_gather(grad_two.astype(jnp.bfloat16))
    down_grad = jnp.dot(activated.T, grad_full, preferred_element_type=jnp.float32)
    grad_pre = jnp.dot(grad_full, down_mat.T, preferred_element_type=jnp.float32) * gelu_slope(
        pre_act
    )
    grad_pre_held = grad_pre.astype(jnp.bfloat16)
    up_grad = jnp.dot(hidden_in.T, grad_pre_held, preferred_element_type=jnp.float32)
    grad_hidden = grad_two + tensor_scatter(jnp.dot(grad_pre_held, up_mat.T, preferred_element_type=jnp.float32).astype(jnp.bfloat16))
    grad_one = norm_back(grad_hidden * params_wide[1], normed_one, scaled_one)
    resid_full = tensor_gather(grad_one.astype(jnp.bfloat16))
    out_grad = jnp.dot(context.T, resid_full, preferred_element_type=jnp.float32)
    grad_context = (
        jnp.dot(resid_full, out_mat.T, preferred_element_type=jnp.float32)
        .astype(jnp.bfloat16)
        .reshape(tokens, head_count, head_size)
    )
    queries = split_heads(qkv_held, 0, head_count, head_size)
    keys = split_heads(qkv_held, 1, head_count, head_size)
    values = split_heads(qkv_held, 2, head_count, head_size)
    same_seq = pack_ids[:, None] == pack_ids[None, :]
    attn_prob = masked_probs(queries, keys, same_seq)
    grad_prob = jnp.einsum("qhd,khd->hqk", grad_context, values, preferred_element_type=jnp.float32)
    row_dots = jnp.sum(attn_prob * grad_prob, axis=-1, keepdims=True)
    grad_scores = (attn_prob * (grad_prob - row_dots) * head_size ** (-0.5)).astype(jnp.bfloat16)
    grad_queries = jnp.einsum("hqk,khd->qhd", grad_scores, keys, preferred_element_type=jnp.float32)
    grad_keys = jnp.einsum("hqk,qhd->khd", grad_scores, queries, preferred_element_type=jnp.float32)
    grad_values = jnp.einsum(
        "hqk,qhd->khd",
        attn_prob.astype(jnp.bfloat16),
        grad_context,
        preferred_element_type=jnp.float32,
    )
    qv_grad = jnp.stack([jnp.sum(grad_queries, axis=0), jnp.sum(grad_values, axis=0)])
    grad_qkv = (
        jnp.stack([grad_queries, grad_keys, grad_values], axis=1)
        .reshape(tokens, 3, width)
        .astype(jnp.bfloat16)
    )
    qkv_grad = jnp.einsum("tc,tjn->jcn", gathered, grad_qkv, preferred_element_type=jnp.float32)
    grad_inputs = grad_one + tensor_scatter(jnp.einsum("tjn,jcn->tc", grad_qkv, qkv_mat, preferred_element_type=jnp.float32).astype(
            jnp.bfloat16
        ))
    row_grads = jnp.stack(
        [
            jnp.sum(grad_one, axis=0),
            jnp.sum(grad_hidden * normed_one, axis=0),
            jnp.sum(grad_hidden, axis=0),
            jnp.sum(grad_two, axis=0),
            jnp.sum(upstream * normed_two, axis=0),
            jnp.sum(upstream, axis=0),
        ]
    )
    up_shift_grad = jnp.sum(grad_pre, axis=0).reshape(up_shift.shape)
    return (
        grad_inputs,
        (qkv_grad, qv_grad, out_grad, up_grad, up_shift_grad, down_grad),
        row_grads,
    )


def shards(
    block_input,
    seq_ids,
    out_cotangent,
    qkv_weight,
    qv_bias,
    out_weight,
    out_bias,
    norm1_gain,
    norm1_bias,
    up_weight,
    up_bias,
    down_weight,
    down_bias,
    norm2_gain,
    norm2_bias,
):
    section = lax.axis_index("section")
    first = section == 0
    dp_count = lax.axis_size("dp")
    line = lax.axis_size("tensor")
    heads, head_part = qv_bias.shape[2], qv_bias.shape[3]
    groups, unit_part = up_bias.shape[1], up_bias.shape[2]
    part = out_bias.shape[1]
    columns = "columns" if part % 128 == 0 else "stack"
    forms = ["rows", columns, "rows", columns, "stack"]

    small_sizes = (qv_bias[0].size, up_bias[0].size, 6 * part)
    small_rows = -(-sum(small_sizes) // 2048) * 16
    small = jnp.concatenate(
        [
            qv_bias.reshape(-1),
            up_bias.reshape(-1),
            out_bias[0],
            norm1_gain[0],
            norm1_bias[0],
            down_bias[0],
            norm2_gain[0],
            norm2_bias[0],
            jnp.zeros((small_rows * 128 - sum(small_sizes),), BF16),
        ]
    ).reshape(small_rows, 128)
    carried = {
        0: ((jnp.swapaxes(qkv_weight[0], 0, 1), out_weight[0], small), ["rows", columns, "stack"]),
        1: ((up_weight[0],), ["rows"]),
        2: ((down_weight[0],), [columns]),
    }
    stacked = {}

    def link_first(number, array):
        if number not in carried:
            return tensor_scatter(array)
        result, stacked[number] = joint_link(number, array, *carried[number])
        return result

    def link_plain(number, array):
        return tensor_scatter(array) if number % 2 else tensor_gather(array)

    def joined(array):
        return array if columns != "stack" else jnp.moveaxis(array, 0, 1).reshape(array.shape[1], -1)

    def layer_weights(which, number):
        if number == 1:
            return stacked[1][0][which]
        if number == 2:
            return joined(stacked[2][0][which])
        qkv_full, out_full, small_full = [array[which] for array in stacked[0]]
        out_full = joined(out_full)
        flat = small_full.reshape(dp_count, -1)
        qv_full = flat[:, : small_sizes[0]].reshape(dp_count, 2, heads, head_part)
        qv_full = jnp.moveaxis(qv_full, 0, 2).reshape(2, heads, dp_count * head_part)
        middle = small_sizes[0] + small_sizes[1]
        up_shift = flat[:, small_sizes[0] : middle].reshape(dp_count, groups, unit_part)
        up_shift = jnp.moveaxis(up_shift, 0, 1).reshape(groups, dp_count * unit_part)
        row_params = flat[:, middle : middle + small_sizes[2]].reshape(dp_count, 6, part)
        row_params = jnp.moveaxis(row_params, 0, 1).reshape(6, dp_count * part)
        return (qkv_full, qv_full, out_full, up_shift, row_params)

    def all_weights(which):
        qkv_mat, qv_shift, out_mat, up_shift, row_params = layer_weights(which, 0)
        up_mat, down_mat = layer_weights(which, 1), layer_weights(which, 2)
        return (qkv_mat, qv_shift, out_mat, up_mat, up_shift, down_mat, row_params)

    rows = jnp.where(first, block_input[0, 0], block_input[1, 0])
    ids = jnp.where(first, seq_ids[0, 0], seq_ids[1, 0])
    upstream = jnp.where(first, out_cotangent[0, 0], out_cotangent[1, 0]).astype(F32)
    out_first, saved_first = layer_forward(rows, ids, link_first, functools.partial(layer_weights, 0))
    out_last, saved_last = layer_forward(
        out_first, ids, link_plain, functools.partial(layer_weights, 1)
    )
    swap = [(0, 1), (1, 0)]
    other_out = lax.ppermute(jnp.where(first, out_last, out_first), "section", swap)
    own_out = jnp.where(first, out_first, out_last)
    section_outputs = jnp.stack(
        [jnp.where(first, own_out, other_out), jnp.where(first, other_out, own_out)]
    )
    grad_last, mats_last, rows_last = layer_backward(upstream, ids, all_weights(1), saved_last)
    grad_first, mats_first, rows_first = layer_backward(grad_last, ids, all_weights(0), saved_first)
    other_grad = lax.ppermute(
        jnp.where(first, grad_last, grad_first).astype(BF16), "section", swap
    ).astype(F32)
    own_grad = jnp.where(first, grad_first, grad_last)
    input_grads = jnp.stack(
        [jnp.where(first, own_grad, other_grad), jnp.where(first, other_grad, own_grad)]
    )

    def blocks(array):
        cut = array.reshape(array.shape[:-1] + (dp_count, array.shape[-1] // dp_count))
        return jnp.moveaxis(cut, -2, 0)

    def padded(flat):
        size = -(-flat.shape[1] // 1024) * 1024
        return jnp.pad(flat, ((0, 0), (0, size - flat.shape[1]))).reshape(dp_count, -1, 128)

    def packed(mats, row_grads):
        qkv_grad, qv_grad, out_grad, up_grad, up_shift_grad, down_grad = mats
        qv_flat = blocks(qv_grad.reshape(2, heads, -1)).reshape(dp_count, -1)
        up_flat = blocks(up_shift_grad).reshape(dp_count, -1)
        bias_flat = padded(jnp.concatenate([qv_flat, up_flat], axis=1))
        row_flat = padded(blocks(row_grads).reshape(dp_count, -1))
        if columns == "stack":
            out_grad, down_grad = blocks(out_grad), blocks(down_grad)
        return (
            qkv_grad.astype(BF16),
            out_grad.astype(BF16),
            up_grad.astype(BF16),
            down_grad.astype(BF16),
            bias_flat,
            row_flat,
        )

    both = [
        jnp.stack(pair) for pair in zip(packed(mats_first, rows_first), packed(mats_last, rows_last))
    ]
    shapes = [
        (3, part, qkv_weight.shape[3]),
        out_weight.shape[1:],
        up_weight.shape[1:],
        down_weight.shape[1:],
        both[4].shape[2:],
        both[5].shape[2:],
    ]
    qkv_sum, out_sum, up_sum, down_sum, bias_sum, _, row_sum = scatter_grads(
        both, forms + ["stack"], shapes
    )
    bias_sum = bias_sum.reshape(-1)
    qv_sum = bias_sum[: small_sizes[0]].reshape(1, 2, heads, head_part)
    up_shift_sum = bias_sum[small_sizes[0] : small_sizes[0] + small_sizes[1]].reshape(
        1, groups, unit_part
    )
    row_sum = row_sum.reshape(-1)[: 6 * part].reshape(6, line, part // line)
    row_sum = lax.dynamic_index_in_dim(row_sum, lax.axis_index("tensor"), 1, keepdims=False)
    return (
        section_outputs[None, :, None],
        input_grads[None, :, None],
        jnp.swapaxes(qkv_sum, 0, 1)[None],
        qv_sum,
        out_sum[None],
        row_sum[0][None],
        row_sum[1][None],
        row_sum[2][None],
        up_sum[None],
        up_shift_sum,
        down_sum[None],
        row_sum[3][None],
        row_sum[4][None],
        row_sum[5][None],
    )


def solution(mesh):
    return jax.shard_map(
        shards,
        mesh=mesh,
        in_specs=(
            P(None, "dp", "tensor", None),
            P(None, "dp", None),
            P(None, "dp", "tensor", None),
            P("section", "dp", None, "tensor"),
            P("section", None, "tensor", "dp"),
            P("section", "tensor", "dp"),
            P("section", "dp"),
            P("section", "dp"),
            P("section", "dp"),
            P("section", "dp", "tensor"),
            P("section", "tensor", "dp"),
            P("section", "tensor", "dp"),
            P("section", "dp"),
            P("section", "dp"),
            P("section", "dp"),
        ),
        out_specs=(
            P("section", None, "dp", "tensor", None),
            P("section", None, "dp", "tensor", None),
            P("section", "dp", None, "tensor"),
            P("section", None, "tensor", "dp"),
            P("section", "tensor", "dp"),
            P("section", ("dp", "tensor")),
            P("section", ("dp", "tensor")),
            P("section", ("dp", "tensor")),
            P("section", "dp", "tensor"),
            P("section", "tensor", "dp"),
            P("section", "tensor", "dp"),
            P("section", ("dp", "tensor")),
            P("section", ("dp", "tensor")),
            P("section", ("dp", "tensor")),
        ),
        check_vma=False,
    )
```
